256 devices in a mesh: section: 8 (over z_hi, x), seq: 32 (over y, z_lo, core).
Axes of the slice: x: 4, y: 4, z: 8 (z_hi: 2, z_lo: 4; z = z_hi * 4 + z_lo), core: 2. Of those that a mesh axis runs over, the one named last changes fastest.
Arguments:
- input_keys: bfloat16 [8, 16384, 2048], P('section', 'seq'), may hold values from -6 to 6
- input_values: bfloat16 [8, 16384, 2048], P('section', 'seq'), may hold values from -6 to 6
- latent_queries: bfloat16 [8, 1024, 2048], P('section', 'seq'), may hold values from -6 to 6
- forward_out: bfloat16 [8, 1024, 2048], P('section', 'seq'), may hold values from -0.59765625 to 0.59765625
- log_norms: float32 [8, 1024, 16], P('section'), as said below
- block_table: int32 [8, 8], P('section'), may hold values from 0 to 127, as said below
- layer_grads: float32 [8, 8, 1024, 2048], P('section', None, 'seq'), may hold values from -600 to 600
Outputs:
- grad_keys: bfloat16 [8, 16384, 2048], P('section', 'seq')
- grad_values: bfloat16 [8, 16384, 2048], P('section', 'seq')
- grad_queries: bfloat16 [8, 1024, 2048], P('section', 'seq')
The draws below stay inside these ranges and needn't reach their ends.
Inputs may be any that keep to these rules, and one draw needn't show every extreme that they name: block_table[b, a] is the last block of 128 input positions that latent block a sees; it rises strictly with a, it lies from 16 * (a + 1) - 8 to 16 * (a + 1) - 1, and the last latent block sees every position. log_norms[b, i, h] stand in for the saved normalizers: they are drawn near the log of the number of positions that latent i sees, plus 0.5, with noise of at most 0.45 either way.
All inputs are finite; a program needn't handle non-finite values.
Results may differ from the reference program's by a relative error of at most 0.0058.
Values may be sent and summed in bfloat16 or wider, within the bound.
No kernel may reach another device: no remote copies, remote signals or barrier semaphores. Data moves between devices by JAX's collectives and lax.ppermute only.
A program may use at most 128 MiB of HBM per device.

```python
import math
import jax
import jax.numpy as jnp
from jax import lax

D = 2048
HEADS = 16
HD = 128
LAT = 1024
BLK = 128
SEQS = 8
TOKENS = 16384
N_SECTION = 8


def block_limits(key):
    table_key = jax.random.fold_in(key, 101)
    total_blocks = TOKENS // BLK
    lat_blocks = LAT // BLK
    spread = max(total_blocks // (2 * lat_blocks), 1)
    jitter = jax.random.randint(table_key, (SEQS, lat_blocks), 0, spread)
    position = jnp.arange(lat_blocks)
    base = total_blocks * (position + 1) // lat_blocks - 1
    limits = jnp.where(position[None, :] == lat_blocks - 1, total_blocks - 1, base[None, :] - jitter)
    return limits.astype(jnp.int32)


def draw_block_table(key, part):
    return block_limits(key)


def draw_log_norms(key, part):
    limits = block_limits(key)
    row_limits = jnp.repeat(limits, BLK, axis=1)
    seen_count = ((row_limits + 1) * BLK).astype(jnp.float32)
    noise_key = jax.random.fold_in(key, 202)
    noise = jnp.clip(0.15 * jax.random.normal(noise_key, (SEQS, LAT, HEADS), jnp.float32), -0.45, 0.45)
    return jnp.log(seen_count)[:, :, None] + 0.5 + noise


def strengthened(entries, key, source, target, parts, factor):
    owner, partner = [(jnp.arange(entries.shape[dim]) // (entries.shape[dim] // parts)).reshape([-1 if axis == dim else 1 for axis in range(entries.ndim)]) for dim in (source, target)]
    chosen = jax.random.permutation(key, parts)[partner]
    strong = (owner == chosen) | (owner == (partner + parts // 2) % parts)
    return jnp.where(strong, factor * entries, entries)


def shard_levels(own_key, shape, cuts, low, high):
    loudness = 1.0
    for dim, blocks in cuts:
        draws = jax.random.uniform(jax.random.fold_in(jax.random.fold_in(own_key, 6), dim), (blocks,), jnp.float32, low / len(cuts), high / len(cuts))
        loudness = loudness * jnp.repeat(jnp.exp(draws), shape[dim] // blocks).reshape((-1,) + (1,) * (len(shape) - 1 - dim))
    return loudness


def bell_draw(stream_key, dims, scale, bound, pieces=(), held_as=jnp.bfloat16):
    drawn = jax.random.normal(stream_key, dims, jnp.float32) * scale
    if len(pieces) > 0:
        drawn = shard_levels(stream_key, dims, pieces, -0.22, 0.18) * drawn
    return jnp.clip(drawn, min=-bound, max=bound).astype(held_as)


def heavy_noise(stream_key, shape, scale, reach, shards, heavy, dtype=jnp.bfloat16):
    result = scale * jax.random.normal(stream_key, shape, jnp.float32)
    if shards:
        result = result * shard_levels(stream_key, shape, shards, -0.22, 0.18)
    return jnp.clip(strengthened(result, jax.random.fold_in(stream_key, 3), *heavy), -reach, reach).astype(dtype)


def setup_inputs(seed: int = 0) -> dict:
    seeds = jax.random.split(jax.random.key(seed), 8)
    return {
        "input_keys": bell_draw(seeds[0], (SEQS, TOKENS, D), 1.0, 6.0, ((0, 8), (1, 32))),
        "input_values": bell_draw(seeds[1], (SEQS, TOKENS, D), 1.0, 6.0, ((0, 8), (1, 32))),
        "latent_queries": bell_draw(seeds[2], (SEQS, LAT, D), 1.0, 6.0, ((0, 8), (1, 32))),
        "forward_out": bell_draw(seeds[3], (SEQS, LAT, D), 0.1, 0.59765625, ((0, 8), (1, 32))),
        "log_norms": draw_log_norms(jax.random.fold_in(seeds[7], 71), 0),
        "block_table": draw_block_table(jax.random.fold_in(seeds[7], 71), 0),
        "layer_grads": heavy_noise(seeds[6], (N_SECTION, SEQS, LAT, D), 100.0, 600.0, ((0, 8), (2, 32)), (0, 1, 8, 2.0), jnp.float32),
    }


def head_terms(queries, grads, delta, lse_rows, key_blk, val_blk, visible, score_scale):
    scores = jnp.dot(queries, key_blk.T, preferred_element_type=jnp.float32) * score_scale
    probs = jnp.where(visible, jnp.exp(scores - lse_rows[:, None]), 0.0)
    probs_low = probs.astype(jnp.bfloat16)
    dprobs = jnp.dot(grads, val_blk.T, preferred_element_type=jnp.float32)
    dscores = (probs * (dprobs - delta[:, None])).astype(jnp.bfloat16)
    query_part = jnp.dot(dscores, key_blk, preferred_element_type=jnp.float32)
    key_part = jnp.dot(dscores.T, queries, preferred_element_type=jnp.float32)
    value_part = jnp.dot(probs_low.T, grads, preferred_element_type=jnp.float32)
    return (query_part, key_part, value_part)

def reference(input_keys, input_values, latent_queries, forward_out, log_norms, block_table, layer_grads):
    score_scale = 1.0 / math.sqrt(HD)
    key_block = jnp.arange(TOKENS) // BLK
    all_keys, all_values, all_queries = ([], [], [])
    for seq_index in range(SEQS):
        out_grad = lax.optimization_barrier(jnp.sum(layer_grads[:, seq_index], axis=0)).astype(jnp.bfloat16)
        limits = jnp.repeat(block_table[seq_index], BLK)
        visible = key_block[None, :] <= limits[:, None]

        def split_heads(array, rows):
            return array.reshape(rows, HEADS, HD).transpose(1, 0, 2)

        def per_head(inputs):
            queries, keys_h, vals_h, grads, outs, lse_rows = inputs
            delta = lax.optimization_barrier(jnp.sum(grads.astype(jnp.float32) * outs.astype(jnp.float32), axis=1))
            query_part, key_part, value_part = head_terms(queries, grads, delta, lse_rows, keys_h, vals_h, visible, score_scale)
            return ((query_part * score_scale).astype(jnp.bfloat16), (key_part * score_scale).astype(jnp.bfloat16), value_part.astype(jnp.bfloat16))
        grad_q, grad_k, grad_v = lax.map(per_head, (split_heads(latent_queries[seq_index], LAT), split_heads(input_keys[seq_index], TOKENS), split_heads(input_values[seq_index], TOKENS), split_heads(out_grad, LAT), split_heads(forward_out[seq_index], LAT), log_norms[seq_index].T))
        all_queries.append(grad_q.transpose(1, 0, 2).reshape(LAT, D))
        all_keys.append(grad_k.transpose(1, 0, 2).reshape(TOKENS, D))
        all_values.append(grad_v.transpose(1, 0, 2).reshape(TOKENS, D))
    return (jnp.stack(all_keys), jnp.stack(all_values), jnp.stack(all_queries))
```

```python
import functools
import math

import jax
import jax.numpy as jnp
from jax import lax
from jax.experimental import pallas as pl
from jax.experimental.pallas import tpu as pltpu
from jax.sharding import Mesh, PartitionSpec as P

SECTION = ("zhi", "x")
SEQ = ("y", "zlo", "core")
BLK = 128
HD = 128
HALF = 1024
HEADS = 8
SCALE = 1.0 / math.sqrt(HD)
EXP_SCALE = SCALE * math.log2(math.e)
FAR = -1e30
BF = jnp.bfloat16
F32 = jnp.float32
NN = (((1,), (0,)), ((), ()))
NT = (((1,), (1,)), ((), ()))
TN = (((0,), (0,)), ((), ()))
NEXT = ((0, 1), (1, 2), (2, 3))


def dot(a, b, dims):
    return lax.dot_general(a, b, dims, preferred_element_type=F32)


def pieces(x):
    hi = lax.reduce_precision(x, 8, 7)
    mid = lax.reduce_precision(x - hi, 8, 7)
    return hi, mid, x - hi - mid


def grad_kernel(info, keep, recv, out, mine, other):
    grad = (keep[...] + recv[...].astype(F32)).astype(BF)
    prod = grad.astype(F32) * out[...].astype(F32)
    rows = grad.shape[0]
    col = lax.broadcasted_iota(jnp.int32, (rows, HD), 1)
    for side in range(2):
        extra = jnp.zeros((rows, HD), F32)
        for head in range(HEADS):
            at = (side * HEADS + head) * HD
            rest = -jnp.sum(prod[:, at : at + HD], axis=1, keepdims=True)
            for piece in range(3):
                part = rest.astype(BF).astype(F32)
                extra = jnp.where(col == piece * HEADS + head, part, extra)
                rest = rest - part
        block = jnp.concatenate([grad[:, side * HALF : (side + 1) * HALF], extra.astype(BF)], 1)

        @pl.when(info[0] == side)
        def _():
            mine[...] = block

        @pl.when(info[0] != side)
        def _():
            other[...] = block


def spread_kernel(rows, sends):
    for place in range(4):
        for side in range(2):
            sends[2 * place + side] = rows[:, side * HALF : (side + 1) * HALF]


def attn_kernel(info, *refs, shifts, first, last, tile, group):
    kv, refs = refs[:4], refs[4:]
    count = len(shifts)
    chunks, refs = [refs[4 * i : 4 * i + 4] for i in range(count)], refs[4 * count :]
    if not first:
        dk_in, dv_in = refs[:2]
        refs = refs[2:]
    outs, refs = refs[: (4 if last else 2)], refs[(4 if last else 2) :]
    dqs, refs = refs[:count], refs[count:]
    q_wide, g_wide = refs
    half = kv[0].shape[0]
    rows = chunks[0][0].shape[0]
    seen = info[1] + shifts[0] < 4

    def put(side, at, cols, dk, dv):
        whole = slice(side * half + at.start, side * half + at.stop)
        if not first:
            dk, dv = (dk_in[whole, cols], dv_in[whole, cols]) if dk is None else (
                dk_in[whole, cols] + dk, dv_in[whole, cols] + dv)
        elif dk is None:
            dk = dv = jnp.zeros((at.stop - at.start, HD), F32)
        if last:
            outs[side][at, cols] = (dk * SCALE).astype(BF)
            outs[2 + side][at, cols] = dv.astype(BF)
        else:
            outs[0][whole, cols] = dk
            outs[1][whole, cols] = dv

    @pl.when(seen)
    def _():
        for sub in range(group):
            cols = slice(sub * HD, (sub + 1) * HD)
            head = pl.program_id(0) * group + sub
            for i, (q, q_extra, g, g_extra) in enumerate(chunks):
                at = slice(i * rows, (i + 1) * rows)
                q_wide[sub, at, :HD] = q[:, cols]
                q_wide[sub, at, HD:] = q_extra[...]
                g_wide[sub, at, :HD] = g[:, cols]
                g_wide[sub, at, HD:] = g_extra[...]
            col = lax.broadcasted_iota(jnp.int32, (BLK, HD), 1)
            total_q = None
            for side in range(2):
                for t in range(half // tile):
                    at = slice(t * tile, (t + 1) * tile)
                    pick = []
                    for j in range(tile // BLK):
                        block = (side * half + at.start) // BLK + j
                        miss = jnp.where(col < 24, (col & 7) - head, (col - 24) - block)
                        pick.append(jnp.where(miss == 0, 1.0, 0.0).astype(BF))
                    pick = jnp.concatenate(pick, 0)
                    k = kv[side][at, cols]
                    v = kv[2 + side][at, cols]
                    scores = dot(jnp.concatenate([k, pick], 1), q_wide[sub], NT)
                    probs = jnp.exp2(scores * EXP_SCALE)
                    dprobs = dot(jnp.concatenate([v, pick], 1), g_wide[sub], NT)
                    dscores = (probs * dprobs).astype(BF)
                    dv = dot(probs.astype(BF), g_wide[sub, :, :HD], NN)
                    dk = dot(dscores, q_wide[sub, :, :HD], NN)
                    put(side, at, cols, dk, dv)
                    part = dot(k, dscores, TN)
                    total_q = part if total_q is None else total_q + part
            for i, dq in enumerate(dqs):
                dq[:, cols] = (total_q[:, i * rows : (i + 1) * rows].T * SCALE).astype(BF)

    @pl.when(jnp.logical_not(seen))
    def _():
        for sub in range(group):
            for side in range(2):
                put(side, slice(0, half), slice(sub * HD, (sub + 1) * HD), None, None)
        for dq in dqs:
            dq[...] = jnp.zeros_like(dq)


def attention(info, kv, chunks, sums, last, tile=512, group=2):
    half = kv[0].shape[0]
    rows = chunks[0][3].shape[0]
    wide = group * HD
    steps = HEADS // group
    own = pl.BlockSpec((half, wide), lambda h, info: (0, info[0] * steps + h))
    one = pl.BlockSpec((half, wide), lambda h, info: (0, h))
    both = pl.BlockSpec((2 * half, wide), lambda h, info: (0, h))
    lat = pl.BlockSpec((rows, wide), lambda h, info: (0, h))
    last_block = pl.BlockSpec((rows, HD), lambda h, info: (0, HEADS))
    in_specs, args = [own, one, own, one], list(kv)
    for shift, q, q_extra, g in chunks:
        in_specs += [
            pl.BlockSpec((rows, wide), lambda h, info, s=shift: ((info[1] + s) % 4, h)),
            pl.BlockSpec((rows, HD), lambda h, info, s=shift: ((info[1] + s) % 4, 0)),
            lat,
            last_block,
        ]
        args += [q, q_extra, g, g]
    aliases = {}
    if sums is not None:
        if not last:
            aliases = {1 + len(args): 0, 2 + len(args): 1}
        in_specs += [both, both]
        args += list(sums)
    shape = lambda r, t: jax.ShapeDtypeStruct((r, HALF), t)
    if last:
        out_specs, out_shape = [one] * 4, [shape(half, BF)] * 4
    else:
        out_specs, out_shape = [both] * 2, [shape(2 * half, F32)] * 2
    out_specs += [lat] * len(chunks)
    out_shape += [shape(rows, BF)] * len(chunks)
    work = len(chunks) * rows * 2 * half * HALF
    kernel = functools.partial(
        attn_kernel,
        shifts=[c[0] for c in chunks],
        first=sums is None,
        last=last,
        tile=tile,
        group=group,
    )
    return pl.pallas_call(
        kernel,
        grid_spec=pltpu.PrefetchScalarGridSpec(
            num_scalar_prefetch=1,
            grid=(steps,),
            in_specs=in_specs,
            out_specs=out_specs,
            scratch_shapes=[pltpu.VMEM((group, len(chunks) * rows, 2 * HD), BF)] * 2,
        ),
        out_shape=out_shape,
        input_output_aliases=aliases,
        compiler_params=pltpu.CompilerParams(
            dimension_semantics=("arbitrary",), vmem_limit_bytes=60 << 20
        ),
        cost_estimate=pl.CostEstimate(
            flops=20 * work, bytes_accessed=16 << 20, transcendentals=work // HD
        ),
        name="attention_backward_" + "_".join(str(c[0]) for c in chunks),
    )(info, *args)


def swap(x, axis):
    return lax.ppermute(x, axis, [(0, 1), (1, 0)])


def exchange(x, axis):
    return lax.all_to_all(x, axis, 0, 0, tiled=True)


def shifted(x, axis, shift):
    return lax.ppermute(x, axis, [((i + shift) % 4, i) for i in range(4)])


def back(pairs):
    return [(b, a) for a, b in pairs]


def body(keys, values, latent_queries, forward_out, log_norms, block_table, layer_grads):
    zhi, x = lax.axis_index("zhi"), lax.axis_index("x")
    y, zlo, core = lax.axis_index("y"), lax.axis_index("zlo"), lax.axis_index("core")
    keys, values, queries = keys[0], values[0], latent_queries[0]
    own_rows, width = queries.shape
    all_rows = log_norms.shape[1]
    y_rows = all_rows // 4
    info = jnp.stack([core, y]).astype(jnp.int32)

    def relative(a, axis):
        a = lax.dynamic_slice_in_dim(jnp.concatenate([a, a], axis), zlo, 4, axis)
        return jnp.where(core == 0, a, jnp.flip(a, axis + 1))

    def joined(mine, there):
        first = jnp.where(core == 0, mine, there)
        second = jnp.where(core == 0, there, mine)
        return jnp.concatenate([first, second], axis=1)[None]

    terms = layer_grads[0].reshape(2, 4, own_rows, width)
    term = lambda j: lax.dynamic_index_in_dim(terms, (x + j) % 4, 1, keepdims=False)
    sends = [term(j).astype(BF) for j in (1, 2, 3)]
    arrived = [shifted(send, "x", 3 - j) for j, send in enumerate(sends)]
    terms = term(0) + sum(a.astype(F32) for a in arrived)
    keep = lax.dynamic_index_in_dim(terms, zhi, 0, keepdims=False)
    sent = lax.dynamic_index_in_dim(terms, 1 - zhi, 0, keepdims=False).astype(BF)
    recv = swap(sent, "zhi")

    other = (1 - core) * HALF
    k_pair = swap(lax.dynamic_slice_in_dim(keys, other, HALF, 1), "core")
    v_pair = swap(lax.dynamic_slice_in_dim(values, other, HALF, 1), "core")

    q_send = pl.pallas_call(
        spread_kernel,
        out_shape=jax.ShapeDtypeStruct((8, own_rows, HALF), BF),
        cost_estimate=pl.CostEstimate(flops=0, bytes_accessed=10 << 16, transcendentals=0),
        name="spread",
    )(queries)
    q_chunk = exchange(q_send, ("zlo", "core")).reshape(4, 2, own_rows, HALF)
    q_chunk = relative(q_chunk, 0).reshape(1, y_rows, HALF)
    q_all = exchange(jnp.broadcast_to(q_chunk, (4, y_rows, HALF)), "y").reshape(all_rows, HALF)

    norms = lax.dynamic_slice_in_dim(log_norms[0], core * HEADS, HEADS, 1) * -math.sqrt(HD)
    limits = jnp.broadcast_to(block_table[0][:, None], (8, BLK)).reshape(all_rows, 1)
    block = (y * 4 + zlo) * 8 + jnp.bitwise_xor(jnp.arange(8), 4 * core)[None, :]
    unseen = jnp.where(block <= limits, 0.0, FAR).astype(F32)
    q_extra = jnp.concatenate(
        [*pieces(norms), unseen, jnp.zeros((all_rows, HD - 32), F32)], axis=1
    ).astype(BF)
    q_extra = relative(q_extra.reshape(4, 4, 2, own_rows, HD), 1).reshape(all_rows, HD)

    recv, k_pair, v_pair, q_extra = lax.optimization_barrier((recv, k_pair, v_pair, q_extra))

    piece = jax.ShapeDtypeStruct((own_rows, HALF + HD), BF)
    mine, other = pl.pallas_call(
        grad_kernel,
        grid_spec=pltpu.PrefetchScalarGridSpec(
            num_scalar_prefetch=1,
            grid=(1,),
            in_specs=[pl.BlockSpec((own_rows, width), lambda i, info: (0, 0))] * 3,
            out_specs=[pl.BlockSpec((own_rows, HALF + HD), lambda i, info: (0, 0))] * 2,
        ),
        out_shape=[piece, piece],
        cost_estimate=pl.CostEstimate(flops=1 << 18, bytes_accessed=1 << 20, transcendentals=0),
        name="out_grad",
    )(info, keep, recv, forward_out[0])
    piece = jnp.concatenate([mine, swap(other, "core")], 0)
    g0 = jnp.concatenate([piece] + [shifted(piece, "zlo", j) for j in (1, 2, 3)], 0)

    g1 = lax.ppermute(g0, "y", back(NEXT))
    g3 = lax.ppermute(g0, "y", [(3, 0)])
    kv = (keys, k_pair, values, v_pair)
    g2 = lax.ppermute(g1, "y", back(NEXT[:2]))
    *sums, dq1, dq3 = attention(
        info, kv, [(1, q_all, q_extra, g1), (3, q_all, q_extra, g3)], None, False
    )
    got1 = lax.ppermute(dq1, "y", NEXT)
    got3 = lax.ppermute(dq3, "y", [(0, 3)])
    *sums, dq2 = attention(info, kv, [(2, q_all, q_extra, g2)], sums, False)

    def sent_along_z(dq):
        dq = dq.reshape(4, 2 * own_rows, HALF)
        return [dq[0]] + [shifted(dq[j], "zlo", 4 - j) for j in (1, 2, 3)]

    def added(parts):
        return sum(p.astype(F32) for p in parts)

    dq2, got1, got3, g0 = lax.optimization_barrier((dq2, got1, got3, g0))
    far = sent_along_z(dq2)
    dk, dk_pair, dv, dv_pair, dq0 = attention(info, kv, [(0, q_all, q_extra, g0)], sums, True)
    far, dq0, dk_pair, dv_pair = lax.optimization_barrier((far, dq0, dk_pair, dv_pair))
    near = sent_along_z(added([dq0, got1, got3]).astype(BF))
    far = lax.ppermute(added(far).astype(BF), "y", [(0, 2), (1, 3)])
    there = [swap(dk_pair, "core"), swap(dv_pair, "core")]
    grad_k, grad_v = joined(dk, there[0]), joined(dv, there[1])
    near, far, grad_k, grad_v = lax.optimization_barrier((near, far, grad_k, grad_v))
    dq = added([*near, far]).astype(BF)
    grad_q = joined(dq[:own_rows], swap(dq[own_rows:], "core"))
    return grad_k, grad_v, grad_q


def solution(mesh):
    parts = Mesh(mesh.devices.reshape(2, 4, 4, 4, 2), SECTION + SEQ)
    rows = P(SECTION, SEQ, None)
    placed = (
        rows, rows, rows, rows, P(SECTION, None, None), P(SECTION, None),
        P(SECTION, None, SEQ, None),
    )
    return jax.shard_map(
        body, mesh=parts, in_specs=placed, out_specs=(rows, rows, rows), check_vma=False
    )
```
